128 devices in a mesh: seq: 16 (over x, z_hi, core), head: 8 (over z_lo, y).
Axes of the slice: x: 4, y: 4, z: 4 (z_hi: 2, z_lo: 2; z = z_hi * 2 + z_lo), core: 2. Of those that a mesh axis runs over, the one named last changes fastest.
Arguments:
- hidden: bfloat16 [8192, 4096], P(('seq', 'head')), may hold values from -6 to 6
- masked: int32 [8192], P(('seq', 'head')), may hold values 0 or 1
- mask_embed: bfloat16 [4096], replicated, may hold values from -6 to 6
- in_gain: float32 [4096], replicated, may hold values from 0.5 to 1.5
- w_gate: bfloat16 [4096, 4096], P(None, 'head'), may hold values from -0.09375 to 0.09375
- w_value: bfloat16 [4096, 4096], P(None, 'head'), may hold values from -0.09375 to 0.09375
- w_step: bfloat16 [4096, 64], P(None, 'head'), may hold values from -0.09375 to 0.09375
- w_bc: bfloat16 [4096, 256], replicated, may hold values from -0.0078125 to 0.0078125
- dt_bias_forward: float32 [64], P('head'), may hold values from -1 to 1
- dt_bias_reverse: float32 [64], P('head'), may hold values from -1 to 1
- rate_forward: float32 [64], P('head'), as said below
- rate_reverse: float32 [64], P('head'), as said below
- skip_forward: float32 [64], P('head'), may hold values from 0.5 to 1.5
- skip_reverse: float32 [64], P('head'), may hold values from 0.5 to 1.5
- out_gain: float32 [4096], P('head'), may hold values from 0.1 to 1.9
- w_out: bfloat16 [4096, 4096], P('head'), may hold values from -0.09375 to 0.09375
Outputs:
- mixed: bfloat16 [8192, 4096], P(('seq', 'head'))
The draws below stay inside these ranges and needn't reach their ends.
Inputs may be any that keep to these rules, and one draw needn't show every extreme that they name: `rate_forward`: positive decay rates of the 64 heads, each at most 0.05 a position. `rate_reverse`: positive decay rates of the 64 heads, each at most 0.05 a position.
All inputs are finite; a program needn't handle non-finite values. No bound on the sum of `masked` on one device may be relied on, other than what follows from the above.
Results may differ from the reference program's by a relative error of at most 0.014.
The reference program's roundings to bfloat16 on the way (of `source` and `normed`) count: a program that leaves them out, or rounds other values in their place, can miss the bound.
Values may be sent and summed in bfloat16 or wider, within the bound.
No kernel may reach another device: no remote copies, remote signals or barrier semaphores. Data moves between devices by JAX's collectives and lax.ppermute only.
A program may use at most 128 MiB of HBM per device.

```python
import math
import jax
import jax.numpy as jnp
from jax import lax

D = 4096
HEADS = 64
HEAD_DIM = 64
STATE = 128
BLOCK = 256
TOKENS = 8192
INNER = 4096


def rates_from(key):
    key_order, key_level = jax.random.split(key, 2)
    order = jax.random.permutation(key_order, HEADS)
    slow_count = HEADS // 2
    slow = order < slow_count
    level = jax.random.uniform(key_level, (HEADS,), jnp.float32)
    fast_rate = jnp.exp(math.log(1.0 / 50.0) + level * (math.log(1.0 / 20.0) - math.log(1.0 / 50.0)))
    slow_rate = jnp.exp(math.log(0.1 / TOKENS) + level * math.log(10.0))
    return jnp.where(slow, slow_rate, fast_rate).astype(jnp.float32)


def draw_rate_forward(key, part):
    return rates_from(jax.random.fold_in(key, 11))


def draw_rate_reverse(key, part):
    return rates_from(jax.random.fold_in(key, 23))


def touch_ends(values, own_key, smallest, largest):
    shape = values.shape
    index_at = [jax.random.randint(jax.random.fold_in(own_key, axis), (), 0, shape[axis]) for axis in range(len(shape))]
    values = values.at[tuple(index_at)].set(smallest)
    longest = shape.index(max(shape))
    index_at[longest] = (index_at[longest] + 1) % shape[longest]
    return values.at[tuple(index_at)].set(largest)


def levels(stream_key, shape, cuts, low, high):
    loudness = 1.0
    for axis_at, parts in cuts:
        heights = jax.random.uniform(jax.random.fold_in(jax.random.fold_in(stream_key, 6), axis_at), (parts,), jnp.float32, low / len(cuts), high / len(cuts))
        loudness = loudness * jnp.repeat(jnp.exp(heights), shape[axis_at] // parts).reshape((-1,) + (1,) * (len(shape) - 1 - axis_at))
    return loudness


def centred(stream_key, dims, scale, reach, cuts=(), held_as=jnp.bfloat16):
    result = scale * jax.random.normal(stream_key, dims, jnp.float32)
    if cuts:
        result = result * levels(stream_key, dims, cuts, -0.22, 0.18)
    return jnp.clip(result, -reach, reach).astype(held_as)


def setup_inputs(seed: int = 0) -> dict:
    key_of = jax.random.split(jax.random.key(seed), 17)
    return {
        "hidden": centred(key_of[0], (TOKENS, D), 1.0, 6.0, ((0, 128),)),
        "masked": touch_ends((jax.random.randint(key_of[1], (TOKENS,), 0, 4) < 1).astype(jnp.int32), jax.random.fold_in(key_of[1], 1), 0, 1),
        "mask_embed": centred(key_of[2], (D,), 1.0, 6.0),
        "in_gain": jnp.clip(1.0 + 0.1 * jax.random.normal(key_of[3], (D,), jnp.float32), 0.5, 1.5),
        "w_gate": centred(key_of[4], (D, INNER), D ** -0.5, 0.09375, ((1, 8),)),
        "w_value": centred(key_of[5], (D, INNER), D ** -0.5, 0.09375, ((1, 8),)),
        "w_step": centred(key_of[6], (D, HEADS), D ** -0.5, 0.09375, ((1, 8),)),
        "w_bc": centred(key_of[7], (D, 2 * STATE), (D * STATE) ** -0.5, 0.0078125),
        "dt_bias_forward": jnp.clip(jax.random.uniform(key_of[8], (HEADS,), jnp.float32, -1.0, 1.0) * levels(key_of[8], (HEADS,), ((0, 8),), -0.4, 0.0), -1.0, 1.0),
        "dt_bias_reverse": jnp.clip(jax.random.uniform(key_of[9], (HEADS,), jnp.float32, -1.0, 1.0) * levels(key_of[9], (HEADS,), ((0, 8),), -0.4, 0.0), -1.0, 1.0),
        "rate_forward": draw_rate_forward(jax.random.fold_in(key_of[16], 71), 0),
        "rate_reverse": draw_rate_reverse(jax.random.fold_in(key_of[16], 71), 0),
        "skip_forward": jnp.clip(0.5 + 1.0 * jax.random.uniform(key_of[12], (HEADS,), jnp.float32) ** levels(key_of[12], (HEADS,), ((0, 8),), -0.2, 0.2), 0.5, 1.5),
        "skip_reverse": jnp.clip(0.5 + 1.0 * jax.random.uniform(key_of[13], (HEADS,), jnp.float32) ** levels(key_of[13], (HEADS,), ((0, 8),), -0.2, 0.2), 0.5, 1.5),
        "out_gain": jnp.clip(1.0 + 0.18 * jax.random.normal(key_of[14], (INNER,), jnp.float32), 0.1, 1.9),
        "w_out": centred(key_of[15], (INNER, D), INNER ** -0.5, 0.09375, ((0, 8),)),
    }


epsilon = 1e-05

def scan_direction(values, b_rows, c_rows, steps_dt, rates, skip_gain):
    total_rows = values.shape[0]
    block_count = total_rows // BLOCK
    heads_all = values.shape[1]
    tri_mask = jnp.arange(BLOCK)[:, None] >= jnp.arange(BLOCK)[None, :]
    log_decay = -rates[None, :] * steps_dt

    def one_block(state, pieces):
        val_blk, b_blk, c_blk, log_blk, step_blk = pieces
        cumul = jnp.cumsum(log_blk, axis=0)
        cumul_heads = cumul.T
        differ = cumul_heads[:, :, None] - cumul_heads[:, None, :]
        weights = jnp.exp(jnp.where(tri_mask[None], differ, -jnp.inf)) * step_blk.T[:, None, :]
        scores = jnp.dot(c_blk, b_blk.T, preferred_element_type=jnp.float32)
        mixing = lax.optimization_barrier((scores[None] * weights).astype(jnp.bfloat16))
        inside = jnp.einsum('hts,shp->thp', mixing.astype(jnp.float32), val_blk.astype(jnp.float32))
        entering = lax.optimization_barrier(state.astype(jnp.bfloat16))
        carried = jnp.einsum('tn,hpn->thp', c_blk.astype(jnp.float32), entering.astype(jnp.float32))
        carried = carried * jnp.exp(cumul)[:, :, None]
        to_end = jnp.exp(cumul[-1][None, :] - cumul) * step_blk
        scaled = lax.optimization_barrier((val_blk.astype(jnp.float32) * to_end[:, :, None]).astype(jnp.bfloat16))
        block_state = jnp.einsum('shp,sn->hpn', scaled.astype(jnp.float32), b_blk.astype(jnp.float32))
        new_state = jnp.exp(cumul[-1])[:, None, None] * state + block_state
        output = inside + carried + skip_gain[None, :, None] * val_blk.astype(jnp.float32)
        return (new_state, output)
    pieces = (values.reshape(block_count, BLOCK, heads_all, HEAD_DIM), b_rows.reshape(block_count, BLOCK, STATE), c_rows.reshape(block_count, BLOCK, STATE), log_decay.reshape(block_count, BLOCK, heads_all), steps_dt.reshape(block_count, BLOCK, heads_all))
    start_state = jnp.zeros((heads_all, HEAD_DIM, STATE), jnp.float32)
    _, outputs = lax.scan(one_block, start_state, pieces)
    return outputs.reshape(total_rows, heads_all * HEAD_DIM)

def gated_norm(output, gate_act, out_gain):
    gated = output * gate_act
    scale = lax.rsqrt(lax.optimization_barrier(jnp.mean(gated * gated, axis=1, keepdims=True)) + epsilon)
    return (gated * scale * out_gain[None, :]).astype(jnp.bfloat16)

def reference(hidden, masked, mask_embed, in_gain, w_gate, w_value, w_step, w_bc, dt_bias_forward, dt_bias_reverse, rate_forward, rate_reverse, skip_forward, skip_reverse, out_gain, w_out):
    source = jnp.where(masked[:, None] == 1, mask_embed[None, :], hidden)
    source_f = source.astype(jnp.float32)
    normed = (source_f * lax.rsqrt(lax.optimization_barrier(jnp.mean(source_f * source_f, axis=1, keepdims=True)) + epsilon) * in_gain[None, :]).astype(jnp.bfloat16)
    gate_proj = jnp.dot(normed, w_gate, preferred_element_type=jnp.float32)
    value_proj = jnp.dot(normed, w_value, preferred_element_type=jnp.float32)
    step_proj = jnp.dot(normed, w_step, preferred_element_type=jnp.float32)
    bc_proj = jnp.dot(normed, w_bc, preferred_element_type=jnp.float32)
    values = jax.nn.silu(value_proj).astype(jnp.bfloat16).reshape(normed.shape[0], HEADS, HEAD_DIM)
    b_rows = bc_proj[:, :STATE].astype(jnp.bfloat16)
    c_rows = bc_proj[:, STATE:].astype(jnp.bfloat16)
    dt_forward = jax.nn.softplus(step_proj + dt_bias_forward[None, :])
    dt_reverse = jax.nn.softplus(step_proj + dt_bias_reverse[None, :])
    forward_out = scan_direction(values, b_rows, c_rows, dt_forward, rate_forward, skip_forward)
    reverse_out = scan_direction(values[::-1], b_rows[::-1], c_rows[::-1], dt_reverse[::-1], rate_reverse, skip_reverse)[::-1]
    gate_act = jax.nn.silu(gate_proj)
    normed_forward = gated_norm(forward_out, gate_act, out_gain)
    normed_reverse = gated_norm(reverse_out, gate_act, out_gain)
    total = jnp.dot(normed_forward, w_out, preferred_element_type=jnp.float32) + jnp.dot(normed_reverse, w_out, preferred_element_type=jnp.float32)
    return total.astype(jnp.bfloat16)
```

```python
import functools

import jax
import jax.numpy as jnp
from jax import lax
from jax.experimental import pallas as pl
from jax.experimental.pallas import tpu as pltpu
from jax.sharding import PartitionSpec as P

HEADS = 64
HEAD_DIM = 64
STATE = 128
BLOCK = 256
EPSILON = 1e-05
OWN = 8
ROWS = 512
PIECE = 64
WIDE = OWN * HEAD_DIM
PAY = STATE + 8

f32 = jnp.float32
bf16 = jnp.bfloat16

MASK = {"A": 1, "B": 3, "Z": 4}
CUT = {"A": (0, 1408), "B": (1408, 2816), "Z": (2816, 4096)}
NEAR, MID, FAR = (1, 3, 4), (2, 7, 5), 6
SLOTS = (0,) + NEAR + MID + (FAR,)


def over(array, dim):
    return lax.ppermute(array, "head", [(i, i ^ MASK[dim]) for i in range(8)])


def along(array, to):
    return lax.ppermute(array, "seq", [(i, to(i)) for i in range(16)])


def dot(a, b):
    return jnp.dot(a, b, preferred_element_type=f32)


def vmem(count):
    return [pl.BlockSpec(memory_space=pltpu.VMEM)] * count


def smem():
    return pl.BlockSpec(memory_space=pltpu.SMEM)


def norm_kernel(hidden, masked, embed, gain, out):
    source = jnp.where(masked[...] == 1, embed[...].astype(f32), hidden[...].astype(f32))
    mean = jnp.mean(source * source, axis=1, keepdims=True)
    out[...] = (source * lax.rsqrt(mean + EPSILON) * gain[...]).astype(bf16)


def input_norm(hidden, masked, embed, gain):
    return pl.pallas_call(
        norm_kernel,
        out_shape=jax.ShapeDtypeStruct(hidden.shape, bf16),
        in_specs=vmem(4),
        out_specs=vmem(1)[0],
        name="input_norm",
    )(hidden, masked[:, None], embed[None, :], gain[None, :])


def softplus(x):
    return jnp.maximum(x, 0.0) + jnp.log1p(jnp.exp(-jnp.abs(x)))


def silu(x):
    return x / (1.0 + jnp.exp(-x))


def pair_lanes(left, right):
    lane = lax.broadcasted_iota(jnp.int32, left.shape, 1)
    return jnp.where(lane < HEAD_DIM, left, right)


def spread(column):
    parts = []
    for q in range(OWN // 2):
        a = jnp.broadcast_to(column[2 * q : 2 * q + 1, :], (1, 128))
        b = jnp.broadcast_to(column[2 * q + 1 : 2 * q + 2, :], (1, 128))
        parts.append(pair_lanes(a, b))
    return jnp.concatenate(parts, axis=1)


def state_kernel(
    head, proj1, proj2, proj3, bias_f, bias_r, rate_f, rate_r,
    pay, values, b_out, c_out, rows_out, cols_out, start_f, start_r, decay_out,
    step_scratch, v3, b3, c3,
):
    me = head[0]
    places = [(proj1, 0), (proj1, 64), (proj1, 128), (proj1, 192), (proj2, 0), (proj2, 64), (proj2, 128), (proj3, 0)]
    for mask, (ref, row) in zip(SLOTS, places, strict=True):
        at = me ^ mask
        v3[at] = silu(ref[row : row + PIECE, 0:WIDE]).astype(bf16)
        b3[at] = ref[row : row + PIECE, WIDE : WIDE + STATE]
        c3[at] = ref[row : row + PIECE, WIDE + STATE : WIDE + 2 * STATE].astype(bf16)
        step_scratch[at] = ref[row : row + PIECE, WIDE + 2 * STATE : WIDE + 3 * STATE]
    values[...] = v3[...].reshape(ROWS, WIDE)
    b_all = b3[...].reshape(ROWS, STATE).astype(bf16)
    b_out[...] = b_all
    c_out[...] = c3[...].reshape(ROWS, STATE)
    steps = step_scratch[...].reshape(ROWS, STATE).T[0:OWN, :]
    dt_f = softplus(steps + bias_f[...])
    dt_r = softplus(steps + bias_r[...])
    cum_f = -rate_f[...] * dt_f
    cum_r = -rate_r[...] * dt_r
    lane = lax.broadcasted_iota(jnp.int32, (OWN, ROWS), 1)
    inner = lane & (BLOCK - 1)
    k = 1
    while k < BLOCK:
        cum_f = cum_f + jnp.where(inner >= k, pltpu.roll(cum_f, k, 1), 0.0)
        cum_r = cum_r + jnp.where(inner < BLOCK - k, pltpu.roll(cum_r, ROWS - k, 1), 0.0)
        k *= 2
    rows = jnp.concatenate([cum_f, cum_r, dt_f, dt_r], axis=0)
    rows_out[...] = rows
    padded = jnp.concatenate([rows, jnp.zeros((STATE - 4 * OWN, ROWS), f32)], axis=0)
    cols_out[...] = padded.T
    tot_f = [cum_f[:, BLOCK - 1 : BLOCK], cum_f[:, ROWS - 1 : ROWS]]
    tot_r = [cum_r[:, 0:1], cum_r[:, BLOCK : BLOCK + 1]]
    first = lane < BLOCK
    end_f = jnp.exp(jnp.where(first, tot_f[0], tot_f[1]) - cum_f) * dt_f
    end_r = jnp.exp(jnp.where(first, tot_r[0], tot_r[1]) - cum_r) * dt_r
    states = []
    for block in range(2):
        span = slice(block * BLOCK, (block + 1) * BLOCK)
        b_t = b_all[span, :].astype(f32).T
        parts_f, parts_r = [], []
        for q in range(OWN // 2):
            lhs = jnp.concatenate(
                [(b_t * end[h : h + 1, span]).astype(bf16) for h in (2 * q, 2 * q + 1) for end in (end_f, end_r)],
                axis=0,
            )
            out = dot(lhs, values[span, q * 128 : (q + 1) * 128])
            parts_f.append(pair_lanes(out[0:128], out[256:384]))
            parts_r.append(pair_lanes(out[128:256], out[384:512]))
        states.append((jnp.concatenate(parts_f, axis=1), jnp.concatenate(parts_r, axis=1)))
    d_f = [spread(jnp.exp(t)) for t in tot_f]
    d_r = [spread(jnp.exp(t)) for t in tot_r]
    start_f[...] = states[0][0]
    start_r[...] = states[1][1]
    decay_out[0:1, :] = d_f[0]
    decay_out[1:2, :] = d_r[1]
    decay_out[2:8, :] = jnp.zeros((6, WIDE), f32)
    pay[0:STATE, :] = (d_f[1] * states[0][0] + states[1][0]).astype(bf16)
    pay[PAY : PAY + STATE, :] = (d_r[0] * states[1][1] + states[0][1]).astype(bf16)
    row = lax.broadcasted_iota(jnp.int32, (8, WIDE), 0)
    for at, total in ((STATE, d_f[0] * d_f[1]), (PAY + STATE, d_r[0] * d_r[1])):
        high = total.astype(bf16).astype(f32)
        tail = jnp.where(row == 0, high, jnp.where(row == 1, total - high, 0.0))
        pay[at : at + 8, :] = tail.astype(bf16)


def piece_states(head, proj1, proj2, proj3, bias_f, bias_r, rate_f, rate_r):
    shapes = [
        ((2 * PAY, WIDE), bf16),
        ((ROWS, WIDE), bf16),
        ((ROWS, STATE), bf16),
        ((ROWS, STATE), bf16),
        ((4 * OWN, ROWS), f32),
        ((ROWS, STATE), f32),
        ((STATE, WIDE), f32),
        ((STATE, WIDE), f32),
        ((8, WIDE), f32),
    ]
    return pl.pallas_call(
        state_kernel,
        out_shape=[jax.ShapeDtypeStruct(s, d) for s, d in shapes],
        in_specs=[smem()] + vmem(7),
        out_specs=vmem(9),
        scratch_shapes=[
            pltpu.VMEM((8, PIECE, STATE), f32),
            pltpu.VMEM((8, PIECE, WIDE), bf16),
            pltpu.VMEM((8, PIECE, STATE), f32),
            pltpu.VMEM((8, PIECE, STATE), bf16),
        ],
        name="piece_states",
    )(head, proj1, proj2, proj3, bias_f[:, None], bias_r[:, None], rate_f[:, None], rate_r[:, None])


def inside_kernel(
    head, gate1, gate2, gate3, values, b_rows, c_rows, rows, cols, skip_f, skip_r,
    base_f, base_r, factor_f, factor_r, g3,
):
    me = head[0]
    places = [(gate1, 0), (gate1, 64), (gate1, 128), (gate1, 192), (gate2, 0), (gate2, 64), (gate2, 128), (gate3, 0)]
    for mask, (ref, row) in zip(SLOTS, places, strict=True):
        g3[me ^ mask] = silu(ref[row : row + PIECE, :])
    below = lax.broadcasted_iota(jnp.int32, (128, 128), 0) >= lax.broadcasted_iota(jnp.int32, (128, 128), 1)
    above = lax.broadcasted_iota(jnp.int32, (128, 128), 0) <= lax.broadcasted_iota(jnp.int32, (128, 128), 1)
    nothing = jnp.zeros((128, 128), bf16)
    for block in range(2):
        lo = block * BLOCK
        span = slice(lo, lo + BLOCK)
        scores = lax.dot_general(
            c_rows[span, :], b_rows[span, :], (((1,), (1,)), ((), ())), preferred_element_type=f32
        )
        gate = g3[4 * block : 4 * block + 4].reshape(BLOCK, WIDE)
        for q in range(OWN // 2):
            lhs, grow = [], []
            for h in (2 * q, 2 * q + 1):
                for way in range(2):
                    at = way * OWN + h
                    col = jnp.broadcast_to(cols[span, at : at + 1], (BLOCK, 128))
                    grow.append(jnp.exp(col))
                    tiles = {}
                    for t, s in (((0, 0), (1, 0), (1, 1)), ((0, 0), (0, 1), (1, 1)))[way]:
                        cut = slice(lo + s * 128, lo + (s + 1) * 128)
                        differ = col[t * 128 : (t + 1) * 128] - rows[at : at + 1, cut]
                        if t == s:
                            differ = jnp.where(above if way else below, differ, -1e30)
                        weight = jnp.exp(differ) * rows[2 * OWN + at : 2 * OWN + at + 1, cut]
                        tiles[t, s] = (scores[t * 128 : (t + 1) * 128, s * 128 : (s + 1) * 128] * weight).astype(bf16)
                    for t in range(2):
                        lhs.append(jnp.concatenate([tiles.get((t, s), nothing) for s in range(2)], axis=1))
            wide = slice(q * 128, (q + 1) * 128)
            value = values[span, wide]
            out = dot(jnp.concatenate(lhs, axis=0), value)
            value = value.astype(f32)
            g = gate[:, wide]
            for way, (base, factor, skip) in enumerate(((base_f, factor_f, skip_f), (base_r, factor_r, skip_r))):
                a, b = way * BLOCK, (2 + way) * BLOCK
                inside = pair_lanes(out[a : a + BLOCK], out[b : b + BLOCK])
                base[span, wide] = (inside + skip[0:1, wide] * value) * g
                factor[span, wide] = pair_lanes(grow[way], grow[2 + way]) * g


def inside_blocks(head, gate1, gate2, gate3, values, b_rows, c_rows, rows, cols, skip_f, skip_r):
    wide = lambda skip: jnp.repeat(skip, HEAD_DIM)[None, :]
    return pl.pallas_call(
        inside_kernel,
        out_shape=[jax.ShapeDtypeStruct((ROWS, WIDE), f32)] * 4,
        in_specs=[smem()] + vmem(10),
        out_specs=vmem(4),
        scratch_shapes=[pltpu.VMEM((8, PIECE, WIDE), f32)],
        name="inside_blocks",
    )(head, gate1, gate2, gate3, values, b_rows, c_rows, rows, cols, wide(skip_f), wide(skip_r))


def split_pay(pay):
    pay = pay.astype(f32)
    return [(pay[at : at + STATE], pay[at + STATE : at + STATE + 1] + pay[at + STATE + 1 : at + STATE + 2]) for at in (0, PAY)]


def join_pay(states):
    parts = []
    for state, decay in states:
        high = lax.reduce_precision(decay, 8, 7)
        zero = jnp.zeros((6, decay.shape[1]), f32)
        parts += [state, high, decay - high, zero]
    return jnp.concatenate(parts, axis=0).astype(bf16)


def then(first, second):
    return second[1] * first[0] + second[0], first[1] * second[1]


def entering_states(pay):
    seq = lax.axis_index("seq")
    core, z, x = seq & 1, (seq >> 1) & 1, seq >> 2
    other = along(pay, lambda i: i ^ 1)
    half = lambda p: jnp.where(core == 0, p[:, : WIDE // 2], p[:, WIDE // 2 :])
    pick = lambda c, a, b: (jnp.where(c, a[0], b[0]), jnp.where(c, a[1], b[1]))

    def both(mine, his, second):
        out = []
        for way in range(2):
            late = (second == 1) if way == 0 else (second == 0)
            out.append(then(pick(late, his[way], mine[way]), pick(late, mine[way], his[way])))
        return out

    chip = both(split_pay(half(pay)), split_pay(half(other)), core)
    beside = split_pay(along(join_pay(chip), lambda i: i ^ 2))
    pair = both(chip, beside, z)
    sent_f, sent_r = join_pay(pair[:1]), join_pay(pair[1:])
    got = []
    for k in (1, 2, 3):
        sent = jnp.where(x + k < 4, sent_f, sent_r)
        arrived = lax.ppermute(sent, "seq", [(i, (i + 4 * k) % 16) for i in range(16)]).astype(f32)
        got.append((arrived[:STATE], arrived[STATE : STATE + 1] + arrived[STATE + 1 : STATE + 2]))
    keep = lambda c, a: jnp.where(c, a, 0.0)
    enter_f = (
        keep(x >= 1, got[0][0])
        + keep(x >= 2, got[0][1] * got[1][0])
        + keep(x >= 3, got[0][1] * got[1][1] * got[2][0])
    )
    enter_r = (
        keep(x <= 2, got[2][0])
        + keep(x <= 1, got[2][1] * got[1][0])
        + keep(x <= 0, got[2][1] * got[1][1] * got[0][0])
    )
    enter_f = jnp.where(z == 1, beside[0][1] * enter_f + beside[0][0], enter_f)
    enter_r = jnp.where(z == 0, beside[1][1] * enter_r + beside[1][0], enter_r)
    mine = jnp.concatenate([enter_f, enter_r], axis=0).astype(bf16)
    return mine, along(mine, lambda i: i ^ 1), other


def gated_kernel(
    where, mine, his, other, start_f, start_r, decay, c_rows, base_f, base_r, factor_f, factor_r, gain,
    out_f, out_r, square, gated3,
):
    me, core = where[0], where[1]
    a, b = mine[...].astype(f32), his[...].astype(f32)
    zero = core == 0
    enter = jnp.concatenate([jnp.where(zero, a, b), jnp.where(zero, b, a)], axis=1)
    enter_f, enter_r = enter[:STATE], enter[STATE:]
    far = lambda at: (other[at : at + STATE, :].astype(f32), other[at + STATE : at + STATE + 1, :].astype(f32) + other[at + STATE + 1 : at + STATE + 2, :].astype(f32))
    state, fade = far(0)
    enter_f = jnp.where(zero, enter_f, fade * enter_f + state)
    state, fade = far(PAY)
    enter_r = jnp.where(zero, fade * enter_r + state, enter_r)
    at_f = (enter_f, decay[0:1, :] * enter_f + start_f[...])
    at_r = (decay[1:2, :] * enter_r + start_r[...], enter_r)
    ones = jnp.ones((8, WIDE), bf16)
    pick = lax.broadcasted_iota(jnp.int32, (8, BLOCK), 0)
    for block in range(2):
        span = slice(block * BLOCK, (block + 1) * BLOCK)
        c_blk = c_rows[span, :]
        sums = []
        for way, (at, base, factor) in enumerate(((at_f, base_f, factor_f), (at_r, base_r, factor_r))):
            gated = base[span, :] + dot(c_blk, at[block].astype(bf16)) * factor[span, :]
            sums.append(
                lax.dot_general(ones, (gated * gated).astype(bf16), (((1,), (1,)), ((), ())), preferred_element_type=f32)
            )
            gated3[way, 4 * block : 4 * block + 4] = (gated * gain[...]).reshape(4, PIECE, WIDE)
        square[:, span] = jnp.where(pick == 0, sums[0], sums[1])
    for slot, mask in enumerate(SLOTS):
        at = me ^ mask
        out_f[slot] = gated3[0, at]
        out_r[slot] = gated3[1, at]


def gated_outputs(where, mine, his, other, start_f, start_r, decay, c_rows, base_f, base_r, factor_f, factor_r, gain):
    return pl.pallas_call(
        gated_kernel,
        out_shape=[
            jax.ShapeDtypeStruct((8, PIECE, WIDE), f32),
            jax.ShapeDtypeStruct((8, PIECE, WIDE), f32),
            jax.ShapeDtypeStruct((8, ROWS), f32),
        ],
        in_specs=[smem()] + vmem(12),
        out_specs=vmem(3),
        scratch_shapes=[pltpu.VMEM((2, 8, PIECE, WIDE), f32)],
        name="gated_outputs",
    )(where, mine, his, other, start_f, start_r, decay, c_rows, base_f, base_r, factor_f, factor_r, gain)


def scale_kernel(head, gated_f, gated_r, square, *refs):
    outs, scale3 = refs[:-1], refs[-1]
    me = head[0]
    scale = lax.rsqrt(square[...] / float(HEADS * HEAD_DIM) + EPSILON)
    padded = jnp.concatenate([scale, jnp.zeros((120, ROWS), f32)], axis=0)
    scale3[...] = padded.T.reshape(8, PIECE, 128)
    slot = 0
    for out in outs:
        for i in range(out.shape[0] // PIECE):
            here = scale3[me ^ SLOTS[slot]]
            out[i * PIECE : (i + 1) * PIECE, :] = (
                gated_f[slot] * here[:, 0:1] + gated_r[slot] * here[:, 1:2]
            ).astype(bf16)
            slot += 1


def scaled_outputs(head, gated_f, gated_r, square):
    return pl.pallas_call(
        scale_kernel,
        out_shape=[jax.ShapeDtypeStruct((n * PIECE, WIDE), bf16) for n in (1, 3, 3, 1)],
        in_specs=[smem()] + vmem(3),
        out_specs=vmem(4),
        scratch_shapes=[pltpu.VMEM((8, PIECE, 128), f32)],
        name="scaled_outputs",
    )(head, gated_f, gated_r, square)


def on_device(
    hidden,
    masked,
    mask_embed,
    in_gain,
    w_gate,
    w_value,
    w_step,
    w_bc,
    dt_bias_forward,
    dt_bias_reverse,
    rate_forward,
    rate_reverse,
    skip_forward,
    skip_reverse,
    out_gain,
    w_out,
):
    me = lax.axis_index("head")
    core = lax.axis_index("seq") & 1
    head = me[None].astype(jnp.int32)
    where = jnp.stack([me, core]).astype(jnp.int32)
    own = input_norm(hidden, masked, mask_embed, in_gain)

    at_a, at_b, at_z = over(own, "A"), over(own, "B"), over(own, "Z")
    at_ab, at_bz, at_za = over(at_b, "A"), over(at_z, "B"), over(at_a, "Z")
    part = lambda array, dim: array[:, slice(*CUT[dim])]
    far = jnp.concatenate(
        [over(part(at_bz, "A"), "A"), over(part(at_za, "B"), "B"), over(part(at_ab, "Z"), "Z")], axis=1
    )
    stages = [
        jnp.concatenate([own, at_a, at_b, at_z], axis=0),
        jnp.concatenate([at_ab, at_bz, at_za], axis=0),
        far,
    ]
    weights = jnp.concatenate([w_value, w_bc, jnp.pad(w_step, ((0, 0), (0, STATE - OWN)))], axis=1)
    proj = [dot(stage, weights) for stage in stages]
    gate = [dot(stage, w_gate) for stage in stages]

    pay, values, b_rows, c_rows, rows, cols, start_f, start_r, decay = piece_states(
        head, *proj, dt_bias_forward, dt_bias_reverse, rate_forward, rate_reverse
    )
    mine, his, other = entering_states(pay)
    base_f, base_r, factor_f, factor_r = inside_blocks(
        head, *gate, values, b_rows, c_rows, rows, cols, skip_forward, skip_reverse
    )
    gated_f, gated_r, square = gated_outputs(
        where, mine, his, other, start_f, start_r, decay, c_rows,
        base_f, base_r, factor_f, factor_r, out_gain[None, :],
    )
    for dim in "ABZ":
        square = square + over(square, dim)
    n_own, n_near, n_mid, n_far = scaled_outputs(head, gated_f, gated_r, square)

    p_far = dot(n_far, w_out).astype(bf16)
    got = {dim: over(part(p_far, dim), dim) for dim in "ABZ"}
    p_mid = dot(n_mid, w_out)

    def with_part(dim_sent, dim_got):
        piece = p_mid[MID.index(dim_sent) * PIECE : (MID.index(dim_sent) + 1) * PIECE]
        a, b = CUT[dim_got]
        middle = piece[:, a:b] + got[dim_got].astype(f32)
        return jnp.concatenate([piece[:, :a], middle, piece[:, b:]], axis=1).astype(bf16)

    got_b = over(with_part(2, "Z"), "A")
    got_z = over(with_part(7, "A"), "B")
    got_a = over(with_part(5, "B"), "Z")
    p_near = dot(n_near, w_out)
    p_own = dot(n_own, w_out)
    near = lambda i, arrived: (p_near[i * PIECE : (i + 1) * PIECE] + arrived.astype(f32)).astype(bf16)
    last = [over(near(0, got_a), "A"), over(near(1, got_b), "B"), over(near(2, got_z), "Z")]
    total = p_own
    for arrived in last:
        total = total + arrived.astype(f32)
    return total.astype(bf16)


def solution(mesh):
    in_specs = (
        P(("seq", "head"), None),
        P(("seq", "head")),
        P(),
        P(),
        P(None, "head"),
        P(None, "head"),
        P(None, "head"),
        P(),
        P("head"),
        P("head"),
        P("head"),
        P("head"),
        P("head"),
        P("head"),
        P("head"),
        P("head", None),
    )
    out_specs = P(("seq", "head"), None)
    return jax.shard_map(
        on_device, mesh=mesh, in_specs=in_specs, out_specs=out_specs, check_vma=False
    )
```

```python
import functools

import jax
import jax.numpy as jnp
from jax import lax
from jax.experimental import pallas as pl
from jax.experimental.pallas import tpu as pltpu
from jax.sharding import PartitionSpec as P


HEADS = 64
HEAD_DIM = 64
STATE = 128
BLOCK = 256
EPSILON = 1e-05
OWN = 8
ROWS = 512
PIECE = 64
WIDE = OWN * HEAD_DIM
PAY = STATE + 8

f32 = jnp.float32
bf16 = jnp.bfloat16

MASK = {"A": 1, "B": 3, "Z": 4}
CUT = {"A": (0, 1408), "B": (1408, 2816), "Z": (2816, 4096)}
NEAR, MID, FAR = (1, 3, 4), (2, 7, 5), 6
SLOTS = (0,) + NEAR + MID + (FAR,)


def over(array, dim):
    return lax.ppermute(array, "head", [(i, i ^ MASK[dim]) for i in range(8)])


def along(array, to):
    return lax.ppermute(array, "seq", [(i, to(i)) for i in range(16)])


def position():
    seq = lax.axis_index("seq")
    return lax.axis_index("head"), seq & 1, (seq >> 1) & 1, seq >> 2


def budget(mib):
    return pltpu.CompilerParams(vmem_limit_bytes=mib << 20)


def dot(a, b):
    return jnp.dot(a, b, preferred_element_type=f32)


def vmem(count):
    return [pl.BlockSpec(memory_space=pltpu.VMEM)] * count


def smem():
    return pl.BlockSpec(memory_space=pltpu.SMEM)


def norm_kernel(hidden, masked, embed, gain, out):
    row = lax.broadcasted_iota(jnp.int32, (PIECE, 128), 0)
    flag = jnp.zeros((PIECE, 128), jnp.int32)
    for i in range(PIECE):
        flag = jnp.where(row == i, masked[i], flag)
    source = jnp.where(flag[:, 0:1] == 1, embed[...].astype(f32)[None, :], hidden[...].astype(f32))
    mean = jnp.mean(source * source, axis=1, keepdims=True)
    out[...] = (source * lax.rsqrt(mean + EPSILON) * gain[...]).astype(bf16)


def input_norm(hidden, masked, embed, gain):
    return pl.pallas_call(
        norm_kernel,
        out_shape=jax.ShapeDtypeStruct(hidden.shape, bf16),
        in_specs=[vmem(1)[0], smem()] + vmem(2),
        out_specs=vmem(1)[0],
        compiler_params=budget(6),
        name="input_norm",
    )(hidden, masked, embed, gain[None, :])


def softplus(x):
    return jnp.maximum(x, 0.0) + jnp.log1p(jnp.exp(-jnp.abs(x)))


def silu(x):
    return x / (1.0 + jnp.exp(-x))


def pair_lanes(left, right):
    lane = lax.broadcasted_iota(jnp.int32, left.shape, 1)
    return jnp.where(lane < HEAD_DIM, left, right)


def heads_column(scalars):
    row = lax.broadcasted_iota(jnp.int32, (OWN, ROWS), 0)
    out = jnp.zeros((OWN, ROWS), f32)
    for h in range(OWN):
        out = jnp.where(row == h, scalars[h], out)
    return out


def heads_row(scalars):
    lane = lax.broadcasted_iota(jnp.int32, (1, WIDE), 1)
    out = jnp.zeros((1, WIDE), f32)
    for h in range(OWN):
        out = jnp.where(lane >= h * HEAD_DIM, scalars[h], out)
    return out


def spread(column):
    parts = []
    for q in range(OWN // 2):
        a = jnp.broadcast_to(column[2 * q : 2 * q + 1, :], (1, 128))
        b = jnp.broadcast_to(column[2 * q + 1 : 2 * q + 2, :], (1, 128))
        parts.append(pair_lanes(a, b))
    return jnp.concatenate(parts, axis=1)


def state_kernel(
    proj1, proj2, proj3, bias_f, bias_r, rate_f, rate_r,
    pay, values, b_out, c_out, rows_out, cols_out, start_f, start_r, decay_out,
    step_scratch, v3, b3, c3,
):
    me = position()[0]
    places = [(proj1, 0), (proj1, 64), (proj1, 128), (proj1, 192), (proj2, 0), (proj2, 64), (proj2, 128), (proj3, 0)]
    for mask, (ref, row) in zip(SLOTS, places, strict=True):
        at = me ^ mask
        v3[at] = silu(ref[row : row + PIECE, 0:WIDE]).astype(bf16)
        b3[at] = ref[row : row + PIECE, WIDE : WIDE + STATE]
        c3[at] = ref[row : row + PIECE, WIDE + STATE : WIDE + 2 * STATE].astype(bf16)
        step_scratch[at] = ref[row : row + PIECE, WIDE + 2 * STATE : WIDE + 3 * STATE]
    values[...] = v3[...].reshape(ROWS, WIDE)
    b_all = b3[...].reshape(ROWS, STATE).astype(bf16)
    b_out[...] = b_all
    c_out[...] = c3[...].reshape(ROWS, STATE)
    steps = step_scratch[...].reshape(ROWS, STATE).T[0:OWN, :]
    dt_f = softplus(steps + heads_column(bias_f))
    dt_r = softplus(steps + heads_column(bias_r))
    cum_f = -heads_column(rate_f) * dt_f
    cum_r = -heads_column(rate_r) * dt_r
    lane = lax.broadcasted_iota(jnp.int32, (OWN, ROWS), 1)
    inner = lane & (BLOCK - 1)
    k = 1
    while k < BLOCK:
        cum_f = cum_f + jnp.where(inner >= k, pltpu.roll(cum_f, k, 1), 0.0)
        cum_r = cum_r + jnp.where(inner < BLOCK - k, pltpu.roll(cum_r, ROWS - k, 1), 0.0)
        k *= 2
    rows = jnp.concatenate([cum_f, cum_r, dt_f, dt_r], axis=0)
    rows_out[...] = rows
    padded = jnp.concatenate([rows, jnp.zeros((STATE - 4 * OWN, ROWS), f32)], axis=0)
    cols_out[...] = padded.T
    tot_f = [cum_f[:, BLOCK - 1 : BLOCK], cum_f[:, ROWS - 1 : ROWS]]
    tot_r = [cum_r[:, 0:1], cum_r[:, BLOCK : BLOCK + 1]]
    first = lane < BLOCK
    end_f = jnp.exp(jnp.where(first, tot_f[0], tot_f[1]) - cum_f) * dt_f
    end_r = jnp.exp(jnp.where(first, tot_r[0], tot_r[1]) - cum_r) * dt_r
    states = []
    for block in range(2):
        span = slice(block * BLOCK, (block + 1) * BLOCK)
        b_t = b_all[span, :].astype(f32).T
        parts_f, parts_r = [], []
        for q in range(OWN // 2):
            lhs = jnp.concatenate(
                [(b_t * end[h : h + 1, span]).astype(bf16) for h in (2 * q, 2 * q + 1) for end in (end_f, end_r)],
                axis=0,
            )
            out = dot(lhs, values[span, q * 128 : (q + 1) * 128])
            parts_f.append(pair_lanes(out[0:128], out[256:384]))
            parts_r.append(pair_lanes(out[128:256], out[384:512]))
        states.append((jnp.concatenate(parts_f, axis=1), jnp.concatenate(parts_r, axis=1)))
    d_f = [spread(jnp.exp(t)) for t in tot_f]
    d_r = [spread(jnp.exp(t)) for t in tot_r]
    start_f[...] = states[0][0]
    start_r[...] = states[1][1]
    decay_out[0:1, :] = d_f[0]
    decay_out[1:2, :] = d_r[1]
    decay_out[2:8, :] = jnp.zeros((6, WIDE), f32)
    pay[0:STATE, :] = (d_f[1] * states[0][0] + states[1][0]).astype(bf16)
    pay[PAY : PAY + STATE, :] = (d_r[0] * states[1][1] + states[0][1]).astype(bf16)
    row = lax.broadcasted_iota(jnp.int32, (8, WIDE), 0)
    for at, total in ((STATE, d_f[0] * d_f[1]), (PAY + STATE, d_r[0] * d_r[1])):
        high = total.astype(bf16).astype(f32)
        tail = jnp.where(row == 0, high, jnp.where(row == 1, total - high, 0.0))
        pay[at : at + 8, :] = tail.astype(bf16)


def piece_states(proj1, proj2, proj3, bias_f, bias_r, rate_f, rate_r):
    shapes = [
        ((2 * PAY, WIDE), bf16),
        ((ROWS, WIDE), bf16),
        ((ROWS, STATE), bf16),
        ((ROWS, STATE), bf16),
        ((4 * OWN, ROWS), f32),
        ((ROWS, STATE), f32),
        ((STATE, WIDE), f32),
        ((STATE, WIDE), f32),
        ((8, WIDE), f32),
    ]
    return pl.pallas_call(
        state_kernel,
        out_shape=[jax.ShapeDtypeStruct(s, d) for s, d in shapes],
        in_specs=vmem(3) + [smem()] * 4,
        out_specs=vmem(9),
        scratch_shapes=[
            pltpu.VMEM((8, PIECE, STATE), f32),
            pltpu.VMEM((8, PIECE, WIDE), bf16),
            pltpu.VMEM((8, PIECE, STATE), f32),
            pltpu.VMEM((8, PIECE, STATE), bf16),
        ],
        compiler_params=budget(14),
        name="piece_states",
    )(proj1, proj2, proj3, bias_f, bias_r, rate_f, rate_r)


def inside_kernel(
    block, gate1, gate2, gate3, values, b_rows, c_rows, rows, cols, skip_f, skip_r,
    base_f, base_r, factor_f, factor_r, g3,
):
    me = position()[0]
    places = [(gate1, 0), (gate1, 64), (gate1, 128), (gate1, 192), (gate2, 0), (gate2, 64), (gate2, 128), (gate3, 0)]
    for mask, (ref, row) in zip(SLOTS, places, strict=True):
        at = (me ^ mask) - 4 * block

        @pl.when((at >= 0) & (at < 4))
        def _(ref=ref, row=row, at=at):
            g3[at] = silu(ref[row : row + PIECE, :])

    below = lax.broadcasted_iota(jnp.int32, (128, 128), 0) >= lax.broadcasted_iota(jnp.int32, (128, 128), 1)
    above = lax.broadcasted_iota(jnp.int32, (128, 128), 0) <= lax.broadcasted_iota(jnp.int32, (128, 128), 1)
    nothing = jnp.zeros((128, 128), bf16)
    skips = heads_row(skip_f), heads_row(skip_r)
    lo = block * BLOCK
    span = slice(lo, lo + BLOCK)
    scores = lax.dot_general(
        c_rows[span, :], b_rows[span, :], (((1,), (1,)), ((), ())), preferred_element_type=f32
    )
    gate = g3[...].reshape(BLOCK, WIDE)
    for q in range(OWN // 2):
        lhs, grow = [], []
        for h in (2 * q, 2 * q + 1):
            for way in range(2):
                at = way * OWN + h
                col = jnp.broadcast_to(cols[span, at : at + 1], (BLOCK, 128))
                grow.append(jnp.exp(col))
                tiles = {}
                for t, s in (((0, 0), (1, 0), (1, 1)), ((0, 0), (0, 1), (1, 1)))[way]:
                    cut = slice(lo + s * 128, lo + (s + 1) * 128)
                    differ = col[t * 128 : (t + 1) * 128] - rows[at : at + 1, cut]
                    if t == s:
                        differ = jnp.where(above if way else below, differ, -1e30)
                    weight = jnp.exp(differ) * rows[2 * OWN + at : 2 * OWN + at + 1, cut]
                    tiles[t, s] = (scores[t * 128 : (t + 1) * 128, s * 128 : (s + 1) * 128] * weight).astype(bf16)
                for t in range(2):
                    lhs.append(jnp.concatenate([tiles.get((t, s), nothing) for s in range(2)], axis=1))
        wide = slice(q * 128, (q + 1) * 128)
        value = values[span, wide]
        out = dot(jnp.concatenate(lhs, axis=0), value)
        value = value.astype(f32)
        g = gate[:, wide]
        for way, (base, factor) in enumerate(((base_f, factor_f), (base_r, factor_r))):
            a, b = way * BLOCK, (2 + way) * BLOCK
            inside = pair_lanes(out[a : a + BLOCK], out[b : b + BLOCK])
            base[:, wide] = (inside + skips[way][:, wide] * value) * g
            factor[:, wide] = pair_lanes(grow[way], grow[2 + way]) * g


def inside_block(block, gate1, gate2, gate3, values, b_rows, c_rows, rows, cols, skip_f, skip_r):
    return pl.pallas_call(
        functools.partial(inside_kernel, block),
        out_shape=[jax.ShapeDtypeStruct((BLOCK, WIDE), f32)] * 4,
        in_specs=vmem(8) + [smem()] * 2,
        out_specs=vmem(4),
        scratch_shapes=[pltpu.VMEM((4, PIECE, WIDE), f32)],
        compiler_params=budget(14),
    )(gate1, gate2, gate3, values, b_rows, c_rows, rows, cols, skip_f, skip_r)


HALF = WIDE // 2


def read_pay(ref, at, lanes=slice(None)):
    tail = ref[at + STATE : at + PAY, lanes].astype(f32)
    return ref[at : at + STATE, lanes].astype(f32), tail[0:1] + tail[1:2]


def write_pay(ref, at, state, decay):
    ref[at : at + STATE, :] = state.astype(bf16)
    row = lax.broadcasted_iota(jnp.int32, (PAY - STATE, state.shape[1]), 0)
    high = decay.astype(bf16).astype(f32)
    tail = jnp.where(row == 0, high, jnp.where(row == 1, decay - high, 0.0))
    ref[at + STATE : at + PAY, :] = tail.astype(bf16)


def choose(cond, a, b):
    return jnp.where(cond, a[0], b[0]), jnp.where(cond, a[1], b[1])


def joined(mine, his, mine_later):
    first, second = choose(mine_later, his, mine), choose(mine_later, mine, his)
    return second[1] * first[0] + second[0], first[1] * second[1]


def chip_kernel(pay, other, out):
    core = position()[1]
    left, right = slice(0, HALF), slice(HALF, WIDE)
    for way, at in enumerate((0, PAY)):
        mine, his = [choose(core == 0, read_pay(p, at, left), read_pay(p, at, right)) for p in (pay, other)]
        write_pay(out, at, *joined(mine, his, core == 1 - way))


def pair_kernel(chip, beside, *outs):
    _, _, z, x = position()
    total = [joined(read_pay(chip, at), read_pay(beside, at), z == 1 - way) for way, at in enumerate((0, PAY))]
    for k, out in enumerate(outs, start=1):
        write_pay(out, 0, *choose(x + k < 4, *total))


def enter_kernel(got1, got2, got3, beside, out):
    _, _, z, x = position()
    got = [read_pay(g, 0) for g in (got1, got2, got3)]
    keep = lambda c, a: jnp.where(c, a, 0.0)
    for way in range(2):
        near, mid, far = got if way == 0 else got[::-1]
        step = x if way == 0 else 3 - x
        enter = keep(step >= 1, near[0])
        enter += keep(step >= 2, near[1] * mid[0])
        enter += keep(step >= 3, near[1] * mid[1] * far[0])
        state, decay = read_pay(beside, way * PAY)
        enter = jnp.where(z == 1 - way, decay * enter + state, enter)
        out[way * STATE : (way + 1) * STATE, :] = enter.astype(bf16)


def small_call(kernel, shapes, *arrays):
    return pl.pallas_call(
        kernel,
        out_shape=[jax.ShapeDtypeStruct(s, bf16) for s in shapes],
        in_specs=vmem(len(arrays)),
        out_specs=vmem(len(shapes)),
        compiler_params=budget(6),
    )(*arrays)


def entering_states(pay):
    other = along(pay, lambda i: i ^ 1)
    (chip,) = small_call(chip_kernel, [(2 * PAY, HALF)], pay, other)
    beside = along(chip, lambda i: i ^ 2)
    sent = small_call(pair_kernel, [(PAY, HALF)] * 3, chip, beside)
    got = []
    for k in (1, 2, 3):
        got.append(lax.ppermute(sent[k - 1], "seq", [(i, (i + 4 * k) % 16) for i in range(16)]))
    (mine,) = small_call(enter_kernel, [(2 * STATE, HALF)], *got, beside)
    return mine, along(mine, lambda i: i ^ 1), other


def gated_kernel(
    mine, his, other, start_f, start_r, decay, c_rows, inside0, inside1, gain,
    out_f, out_r, far, square, gated3,
):
    me, core, _, _ = position()
    a, b = mine[...].astype(f32), his[...].astype(f32)
    zero = core == 0
    enter = jnp.concatenate([jnp.where(zero, a, b), jnp.where(zero, b, a)], axis=1)
    enter_f, enter_r = enter[:STATE], enter[STATE:]
    state, fade = read_pay(other, 0)
    enter_f = jnp.where(zero, enter_f, fade * enter_f + state)
    state, fade = read_pay(other, PAY)
    enter_r = jnp.where(zero, fade * enter_r + state, enter_r)
    at_f = (enter_f, decay[0:1, :] * enter_f + start_f[...])
    at_r = (decay[1:2, :] * enter_r + start_r[...], enter_r)
    ones = jnp.ones((8, WIDE), bf16)
    pick = lax.broadcasted_iota(jnp.int32, (8, BLOCK), 0)
    for block in range(2):
        span = slice(block * BLOCK, (block + 1) * BLOCK)
        c_blk = c_rows[span, :]
        base_f, base_r, factor_f, factor_r = (inside0, inside1)[block]
        sums = []
        for way, (at, base, factor) in enumerate(((at_f, base_f, factor_f), (at_r, base_r, factor_r))):
            gated = base[...] + dot(c_blk, at[block].astype(bf16)) * factor[...]
            sums.append(
                lax.dot_general(ones, (gated * gated).astype(bf16), (((1,), (1,)), ((), ())), preferred_element_type=f32)
            )
            gated3[way, 4 * block : 4 * block + 4] = (gated * gain[...]).reshape(4, PIECE, WIDE)
        square[:, span] = jnp.where(pick == 0, sums[0], sums[1])
    for slot, mask in enumerate(SLOTS):
        at = me ^ mask
        out_f[slot] = gated3[0, at]
        out_r[slot] = gated3[1, at]
    far[0:PIECE, :] = out_f[7].astype(bf16)
    far[PIECE : 2 * PIECE, :] = out_r[7].astype(bf16)


def gated_outputs(mine, his, other, start_f, start_r, decay, c_rows, inside0, inside1, gain):
    def kernel(a, b, c, d, e, f, g, *refs):
        gated_kernel(a, b, c, d, e, f, g, refs[0:4], refs[4:8], *refs[8:])

    return pl.pallas_call(
        kernel,
        out_shape=[
            jax.ShapeDtypeStruct((8, PIECE, WIDE), f32),
            jax.ShapeDtypeStruct((8, PIECE, WIDE), f32),
            jax.ShapeDtypeStruct((2 * PIECE, WIDE), bf16),
            jax.ShapeDtypeStruct((8, ROWS), f32),
        ],
        in_specs=vmem(16),
        out_specs=vmem(4),
        scratch_shapes=[pltpu.VMEM((2, 8, PIECE, WIDE), f32)],
        compiler_params=budget(16),
        name="gated_outputs",
    )(mine, his, other, start_f, start_r, decay, c_rows, *inside0, *inside1, gain)


def scale_kernel(gated_f, gated_r, square, *refs):
    outs, scale_out, scale3 = refs[:-2], refs[-2], refs[-1]
    me = position()[0]
    scale = lax.rsqrt(square[...] / float(HEADS * HEAD_DIM) + EPSILON)
    padded = jnp.concatenate([scale, jnp.zeros((120, ROWS), f32)], axis=0)
    scale3[...] = padded.T.reshape(8, PIECE, 128)
    slot = 0
    for out in outs:
        for i in range(out.shape[0] // PIECE):
            here = scale3[me ^ SLOTS[slot]]
            scale_out[slot] = here
            out[i * PIECE : (i + 1) * PIECE, :] = (
                gated_f[slot] * here[:, 0:1] + gated_r[slot] * here[:, 1:2]
            ).astype(bf16)
            slot += 1


def scaled_outputs(gated_f, gated_r, square):
    return pl.pallas_call(
        scale_kernel,
        out_shape=[jax.ShapeDtypeStruct((n * PIECE, WIDE), bf16) for n in (1, 3, 3)]
        + [jax.ShapeDtypeStruct((7, PIECE, 128), f32)],
        in_specs=vmem(3),
        out_specs=vmem(4),
        scratch_shapes=[pltpu.VMEM((8, PIECE, 128), f32)],
        compiler_params=budget(10),
        name="scaled_outputs",
    )(gated_f, gated_r, square)


def on_device(
    hidden,
    masked,
    mask_embed,
    in_gain,
    w_gate,
    w_value,
    w_step,
    w_bc,
    dt_bias_forward,
    dt_bias_reverse,
    rate_forward,
    rate_reverse,
    skip_forward,
    skip_reverse,
    out_gain,
    w_out,
):
    own = input_norm(hidden, masked, mask_embed, in_gain)

    def send(dim, array):
        return over(array, dim)

    at_a, at_b, at_z = [send(dim, own) for dim in "ABZ"]
    at_za = send("Z", at_a)
    at_bz = send("B", at_z)
    at_ab = send("A", at_b)
    part = lambda array, dim: array[:, slice(*CUT[dim])]
    far = [send(dim, part(array, dim)) for dim, array in (("A", at_bz), ("B", at_za), ("Z", at_ab))]
    weights = jnp.concatenate([w_value, w_bc, jnp.pad(w_step, ((0, 0), (0, STATE - OWN)))], axis=1)
    proj, gate = [], []
    for i, blocks in enumerate(((own, at_a, at_b, at_z), (at_ab, at_bz, at_za), far), start=1):
        stage = jnp.concatenate(blocks, axis=0 if i < 3 else 1)
        proj.append(dot(stage, weights))
        gate.append(dot(stage, w_gate))

    pay, values, b_rows, c_rows, rows, cols, start_f, start_r, decay = piece_states(
        *proj, dt_bias_forward, dt_bias_reverse, rate_forward, rate_reverse
    )
    mine, his, other = entering_states(pay)
    inside = []
    for block in range(2):
        inside.append(
            inside_block(block, *gate, values, b_rows, c_rows, rows, cols, skip_forward, skip_reverse)
        )
    gated_f, gated_r, far, square = gated_outputs(
        mine, his, other, start_f, start_r, decay, c_rows, *inside, out_gain[None, :]
    )
    p_far = dot(far, w_out).astype(bf16)
    got = {dim: send(dim, part(p_far, dim)) for dim in "ABZ"}
    for dim in "ABZ":
        square = square + send(dim, square)
    n_own, n_near, n_mid, scale = scaled_outputs(gated_f, gated_r, square)
    p_mid = dot(n_mid, w_out)

    def with_part(mask, dim):
        i = MID.index(mask)
        piece, here = p_mid[i * PIECE : (i + 1) * PIECE], scale[4 + i]
        a, b = CUT[dim]
        arrived = got[dim].astype(f32)
        arrived = arrived[:PIECE] * here[:, 0:1] + arrived[PIECE:] * here[:, 1:2]
        return jnp.concatenate([piece[:, :a], piece[:, a:b] + arrived, piece[:, b:]], axis=1).astype(bf16)

    got_b = send("A", with_part(2, "Z"))
    got_z = send("B", with_part(7, "A"))
    got_a = send("Z", with_part(5, "B"))
    p_near = dot(n_near, w_out)
    p_near = lax.optimization_barrier([p_near[i * PIECE : (i + 1) * PIECE] for i in range(3)])
    total = dot(n_own, w_out)
    near = lambda i, arrived: (p_near[i] + arrived.astype(f32)).astype(bf16)
    last = [send("A", near(0, got_a)), send("B", near(1, got_b)), send("Z", near(2, got_z))]
    for arrived in last:
        total = total + arrived.astype(f32)
    return total.astype(bf16)


def solution(mesh):
    in_specs = (
        P(("seq", "head"), None),
        P(("seq", "head")),
        P(),
        P(),
        P(None, "head"),
        P(None, "head"),
        P(None, "head"),
        P(),
        P("head"),
        P("head"),
        P("head"),
        P("head"),
        P("head"),
        P("head"),
        P("head"),
        P("head", None),
    )
    out_specs = P(("seq", "head"), None)
    return jax.shard_map(on_device, mesh=mesh, in_specs=in_specs, out_specs=out_specs, check_vma=False)
```

```python
import functools

import jax
import jax.numpy as jnp
from jax import lax
from jax.experimental import pallas as pl
from jax.experimental.pallas import tpu as pltpu
from jax.sharding import PartitionSpec as P


HEADS = 64
HEAD_DIM = 64
STATE = 128
BLOCK = 256
EPSILON = 1e-05
OWN = 8
ROWS = 512
PIECE = 64
WIDE = OWN * HEAD_DIM
PAY = STATE + 8

f32 = jnp.float32
bf16 = jnp.bfloat16

MASK = {"A": 1, "B": 3, "Z": 4}
LAST = {"B": (0, 2176), "A": (2176, 4096)}
FIRST = {"A": (0, 2176), "B": (2176, 3584), "Z": (3584, 4096)}
NEAR, MID, FAR = (1, 3, 4), (2, 7, 5), 6
SLOTS = (0,) + NEAR + MID + (FAR,)


def over(array, dim):
    return lax.ppermute(array, "head", [(i, i ^ MASK[dim]) for i in range(8)])


def along(array, to):
    return lax.ppermute(array, "seq", [(i, to(i)) for i in range(16)])


def position():
    seq = lax.axis_index("seq")
    return lax.axis_index("head"), seq & 1, (seq >> 1) & 1, seq >> 2


def budget(mib):
    return pltpu.CompilerParams(vmem_limit_bytes=mib << 20)


def dot(a, b):
    return jnp.dot(a, b, preferred_element_type=f32)


def vmem(count):
    return [pl.BlockSpec(memory_space=pltpu.VMEM)] * count


def smem():
    return pl.BlockSpec(memory_space=pltpu.SMEM)


def norm_kernel(masked, hidden, embed, gain, out):
    row = lax.broadcasted_iota(jnp.int32, (PIECE, 128), 0)
    flag = jnp.zeros((PIECE, 128), jnp.int32)
    for i in range(PIECE):
        flag = jnp.where(row == i, masked[i], flag)
    source = jnp.where(flag[:, 0:1] == 1, embed[...].astype(f32)[None, :], hidden[...].astype(f32))
    mean = jnp.mean(source * source, axis=1, keepdims=True)
    out[...] = (source * lax.rsqrt(mean + EPSILON) * gain[...][None, :]).astype(bf16)


def input_norm(hidden, masked, embed, gain):
    return pl.pallas_call(
        norm_kernel,
        out_shape=jax.ShapeDtypeStruct(hidden.shape, bf16),
        in_specs=[smem()] + vmem(3),
        out_specs=vmem(1)[0],
        compiler_params=budget(60),
        name="input_norm",
    )(masked, hidden, embed, gain)


def softplus(x):
    return jnp.maximum(x, 0.0) + jnp.log1p(jnp.exp(-jnp.abs(x)))


def silu(x):
    return x / (1.0 + jnp.exp(-x))


def pair_lanes(left, right):
    lane = lax.broadcasted_iota(jnp.int32, left.shape, 1)
    return jnp.where(lane < HEAD_DIM, left, right)


def heads_column(scalars):
    row = lax.broadcasted_iota(jnp.int32, (OWN, ROWS), 0)
    out = jnp.zeros((OWN, ROWS), f32)
    for h in range(OWN):
        out = jnp.where(row == h, scalars[h], out)
    return out


def heads_row(scalars):
    lane = lax.broadcasted_iota(jnp.int32, (1, WIDE), 1)
    out = jnp.zeros((1, WIDE), f32)
    for h in range(OWN):
        out = jnp.where(lane >= h * HEAD_DIM, scalars[h], out)
    return out


def spread(column):
    parts = []
    for q in range(OWN // 2):
        a = jnp.broadcast_to(column[2 * q : 2 * q + 1, :], (1, 128))
        b = jnp.broadcast_to(column[2 * q + 1 : 2 * q + 2, :], (1, 128))
        parts.append(pair_lanes(a, b))
    return jnp.concatenate(parts, axis=1)


def state_kernel(
    proj1, proj2, proj3, bias_f, bias_r, rate_f, rate_r,
    pay, values, b_out, c_out, rows_out, cols_out, start_f, start_r, decay_out,
    step_scratch, v3, b3, c3,
):
    me = position()[0]
    places = [(proj1, 0), (proj1, 64), (proj1, 128), (proj1, 192), (proj2, 0), (proj2, 64), (proj2, 128), (proj3, 0)]
    for mask, (ref, row) in zip(SLOTS, places, strict=True):
        at = me ^ mask
        v3[at] = silu(ref[row : row + PIECE, 0:WIDE]).astype(bf16)
        b3[at] = ref[row : row + PIECE, WIDE : WIDE + STATE]
        c3[at] = ref[row : row + PIECE, WIDE + STATE : WIDE + 2 * STATE].astype(bf16)
        step_scratch[at] = ref[row : row + PIECE, WIDE + 2 * STATE : WIDE + 3 * STATE]
    values[...] = v3[...].reshape(ROWS, WIDE)
    b_all = b3[...].reshape(ROWS, STATE).astype(bf16)
    b_out[...] = b_all
    c_out[...] = c3[...].reshape(ROWS, STATE)
    steps = step_scratch[...].reshape(ROWS, STATE).T[0:OWN, :]
    dt_f = softplus(steps + heads_column(bias_f))
    dt_r = softplus(steps + heads_column(bias_r))
    cum_f = -heads_column(rate_f) * dt_f
    cum_r = -heads_column(rate_r) * dt_r
    lane = lax.broadcasted_iota(jnp.int32, (OWN, ROWS), 1)
    inner = lane & (BLOCK - 1)
    k = 1
    while k < BLOCK:
        cum_f = cum_f + jnp.where(inner >= k, pltpu.roll(cum_f, k, 1), 0.0)
        cum_r = cum_r + jnp.where(inner < BLOCK - k, pltpu.roll(cum_r, ROWS - k, 1), 0.0)
        k *= 2
    rows = jnp.concatenate([cum_f, cum_r, dt_f, dt_r], axis=0)
    rows_out[...] = rows
    padded = jnp.concatenate([rows, jnp.zeros((STATE - 4 * OWN, ROWS), f32)], axis=0)
    cols_out[...] = padded.T
    tot_f = [cum_f[:, BLOCK - 1 : BLOCK], cum_f[:, ROWS - 1 : ROWS]]
    tot_r = [cum_r[:, 0:1], cum_r[:, BLOCK : BLOCK + 1]]
    first = lane < BLOCK
    end_f = jnp.exp(jnp.where(first, tot_f[0], tot_f[1]) - cum_f) * dt_f
    end_r = jnp.exp(jnp.where(first, tot_r[0], tot_r[1]) - cum_r) * dt_r
    states = []
    for block in range(2):
        span = slice(block * BLOCK, (block + 1) * BLOCK)
        b_t = b_all[span, :].astype(f32).T
        parts_f, parts_r = [], []
        for q in range(OWN // 2):
            lhs = jnp.concatenate(
                [(b_t * end[h : h + 1, span]).astype(bf16) for h in (2 * q, 2 * q + 1) for end in (end_f, end_r)],
                axis=0,
            )
            out = dot(lhs, values[span, q * 128 : (q + 1) * 128])
            parts_f.append(pair_lanes(out[0:128], out[256:384]))
            parts_r.append(pair_lanes(out[128:256], out[384:512]))
        states.append((jnp.concatenate(parts_f, axis=1), jnp.concatenate(parts_r, axis=1)))
    d_f = [spread(jnp.exp(t)) for t in tot_f]
    d_r = [spread(jnp.exp(t)) for t in tot_r]
    start_f[...] = states[0][0]
    start_r[...] = states[1][1]
    decay_out[0:1, :] = d_f[0]
    decay_out[1:2, :] = d_r[1]
    decay_out[2:8, :] = jnp.zeros((6, WIDE), f32)
    pay[0:STATE, :] = (d_f[1] * states[0][0] + states[1][0]).astype(bf16)
    pay[PAY : PAY + STATE, :] = (d_r[0] * states[1][1] + states[0][1]).astype(bf16)
    row = lax.broadcasted_iota(jnp.int32, (8, WIDE), 0)
    for at, total in ((STATE, d_f[0] * d_f[1]), (PAY + STATE, d_r[0] * d_r[1])):
        high = total.astype(bf16).astype(f32)
        tail = jnp.where(row == 0, high, jnp.where(row == 1, total - high, 0.0))
        pay[at : at + 8, :] = tail.astype(bf16)


def piece_states(proj1, proj2, proj3, bias_f, bias_r, rate_f, rate_r):
    shapes = [
        ((2 * PAY, WIDE), bf16),
        ((ROWS, WIDE), bf16),
        ((ROWS, STATE), bf16),
        ((ROWS, STATE), bf16),
        ((4 * OWN, ROWS), f32),
        ((ROWS, STATE), f32),
        ((STATE, WIDE), f32),
        ((STATE, WIDE), f32),
        ((8, WIDE), f32),
    ]
    return pl.pallas_call(
        state_kernel,
        out_shape=[jax.ShapeDtypeStruct(s, d) for s, d in shapes],
        in_specs=vmem(3) + [smem()] * 4,
        out_specs=vmem(9),
        scratch_shapes=[
            pltpu.VMEM((8, PIECE, STATE), f32),
            pltpu.VMEM((8, PIECE, WIDE), bf16),
            pltpu.VMEM((8, PIECE, STATE), f32),
            pltpu.VMEM((8, PIECE, STATE), bf16),
        ],
        compiler_params=budget(14),
        name="piece_states",
    )(proj1, proj2, proj3, bias_f, bias_r, rate_f, rate_r)


def inside_kernel(
    block, gate1, gate2, gate3, values, b_rows, c_rows, rows, cols, skip_f, skip_r,
    base_f, base_r, factor_f, factor_r, g3,
):
    me = position()[0]
    places = [(gate1, 0), (gate1, 64), (gate1, 128), (gate1, 192), (gate2, 0), (gate2, 64), (gate2, 128), (gate3, 0)]
    for mask, (ref, row) in zip(SLOTS, places, strict=True):
        at = (me ^ mask) - 4 * block

        @pl.when((at >= 0) & (at < 4))
        def _(ref=ref, row=row, at=at):
            g3[at] = silu(ref[row : row + PIECE, :])

    below = lax.broadcasted_iota(jnp.int32, (128, 128), 0) >= lax.broadcasted_iota(jnp.int32, (128, 128), 1)
    above = lax.broadcasted_iota(jnp.int32, (128, 128), 0) <= lax.broadcasted_iota(jnp.int32, (128, 128), 1)
    nothing = jnp.zeros((128, 128), bf16)
    skips = heads_row(skip_f), heads_row(skip_r)
    lo = block * BLOCK
    span = slice(lo, lo + BLOCK)
    scores = lax.dot_general(
        c_rows[span, :], b_rows[span, :], (((1,), (1,)), ((), ())), preferred_element_type=f32
    )
    gate = g3[...].reshape(BLOCK, WIDE)
    for q in range(OWN // 2):
        lhs, grow = [], []
        for h in (2 * q, 2 * q + 1):
            for way in range(2):
                at = way * OWN + h
                col = jnp.broadcast_to(cols[span, at : at + 1], (BLOCK, 128))
                grow.append(jnp.exp(col))
                tiles = {}
                for t, s in (((0, 0), (1, 0), (1, 1)), ((0, 0), (0, 1), (1, 1)))[way]:
                    cut = slice(lo + s * 128, lo + (s + 1) * 128)
                    differ = col[t * 128 : (t + 1) * 128] - rows[at : at + 1, cut]
                    if t == s:
                        differ = jnp.where(above if way else below, differ, -1e30)
                    weight = jnp.exp(differ) * rows[2 * OWN + at : 2 * OWN + at + 1, cut]
                    tiles[t, s] = (scores[t * 128 : (t + 1) * 128, s * 128 : (s + 1) * 128] * weight).astype(bf16)
                for t in range(2):
                    lhs.append(jnp.concatenate([tiles.get((t, s), nothing) for s in range(2)], axis=1))
        wide = slice(q * 128, (q + 1) * 128)
        value = values[span, wide]
        out = dot(jnp.concatenate(lhs, axis=0), value)
        value = value.astype(f32)
        g = gate[:, wide]
        for way, (base, factor) in enumerate(((base_f, factor_f), (base_r, factor_r))):
            a, b = way * BLOCK, (2 + way) * BLOCK
            inside = pair_lanes(out[a : a + BLOCK], out[b : b + BLOCK])
            base[:, wide] = (inside + skips[way][:, wide] * value) * g
            factor[:, wide] = pair_lanes(grow[way], grow[2 + way]) * g


def inside_block(block, gate1, gate2, gate3, values, b_rows, c_rows, rows, cols, skip_f, skip_r):
    return pl.pallas_call(
        functools.partial(inside_kernel, block),
        out_shape=[jax.ShapeDtypeStruct((BLOCK, WIDE), f32)] * 4,
        in_specs=vmem(8) + [smem()] * 2,
        out_specs=vmem(4),
        scratch_shapes=[pltpu.VMEM((4, PIECE, WIDE), f32)],
        compiler_params=budget(14),
    )(gate1, gate2, gate3, values, b_rows, c_rows, rows, cols, skip_f, skip_r)


HALF = WIDE // 2


def read_pay(ref, at, lanes=slice(None)):
    tail = ref[at + STATE : at + PAY, lanes].astype(f32)
    return ref[at : at + STATE, lanes].astype(f32), tail[0:1] + tail[1:2]


def write_pay(ref, at, state, decay):
    ref[at : at + STATE, :] = state.astype(bf16)
    row = lax.broadcasted_iota(jnp.int32, (PAY - STATE, state.shape[1]), 0)
    high = decay.astype(bf16).astype(f32)
    tail = jnp.where(row == 0, high, jnp.where(row == 1, decay - high, 0.0))
    ref[at + STATE : at + PAY, :] = tail.astype(bf16)


def choose(cond, a, b):
    return jnp.where(cond, a[0], b[0]), jnp.where(cond, a[1], b[1])


def joined(mine, his, mine_later):
    first, second = choose(mine_later, his, mine), choose(mine_later, mine, his)
    return second[1] * first[0] + second[0], first[1] * second[1]


def chip_kernel(pay, other, out):
    core = position()[1]
    left, right = slice(0, HALF), slice(HALF, WIDE)
    for way, at in enumerate((0, PAY)):
        mine, his = [choose(core == 0, read_pay(p, at, left), read_pay(p, at, right)) for p in (pay, other)]
        write_pay(out, at, *joined(mine, his, core == 1 - way))


def pair_kernel(chip, beside, *outs):
    _, _, z, x = position()
    total = [joined(read_pay(chip, at), read_pay(beside, at), z == 1 - way) for way, at in enumerate((0, PAY))]
    for k, out in enumerate(outs, start=1):
        write_pay(out, 0, *choose(x + k < 4, *total))


def enter_kernel(got1, got2, got3, beside, out):
    _, _, z, x = position()
    got = [read_pay(g, 0) for g in (got1, got2, got3)]
    keep = lambda c, a: jnp.where(c, a, 0.0)
    for way in range(2):
        near, mid, far = got if way == 0 else got[::-1]
        step = x if way == 0 else 3 - x
        enter = keep(step >= 1, near[0])
        enter += keep(step >= 2, near[1] * mid[0])
        enter += keep(step >= 3, near[1] * mid[1] * far[0])
        state, decay = read_pay(beside, way * PAY)
        enter = jnp.where(z == 1 - way, decay * enter + state, enter)
        out[way * STATE : (way + 1) * STATE, :] = enter.astype(bf16)


def small_call(kernel, shapes, *arrays):
    return pl.pallas_call(
        kernel,
        out_shape=[jax.ShapeDtypeStruct(s, bf16) for s in shapes],
        in_specs=vmem(len(arrays)),
        out_specs=vmem(len(shapes)),
        compiler_params=budget(6),
    )(*arrays)


def entering_states(pay):
    other = along(pay, lambda i: i ^ 1)
    (chip,) = small_call(chip_kernel, [(2 * PAY, HALF)], pay, other)
    beside = along(chip, lambda i: i ^ 2)
    sent = small_call(pair_kernel, [(PAY, HALF)] * 3, chip, beside)
    got = []
    for k in (1, 2, 3):
        got.append(lax.ppermute(sent[k - 1], "seq", [(i, (i + 4 * k) % 16) for i in range(16)]))
    (mine,) = small_call(enter_kernel, [(2 * STATE, HALF)], *got, beside)
    return mine, along(mine, lambda i: i ^ 1), other


def gated_kernel(
    mine, his, other, start_f, start_r, decay, c_rows, inside0, inside1, gain,
    out_f, out_r, far, square, gated3,
):
    me, core, _, _ = position()
    a, b = mine[...].astype(f32), his[...].astype(f32)
    zero = core == 0
    enter = jnp.concatenate([jnp.where(zero, a, b), jnp.where(zero, b, a)], axis=1)
    enter_f, enter_r = enter[:STATE], enter[STATE:]
    state, fade = read_pay(other, 0)
    enter_f = jnp.where(zero, enter_f, fade * enter_f + state)
    state, fade = read_pay(other, PAY)
    enter_r = jnp.where(zero, fade * enter_r + state, enter_r)
    at_f = (enter_f, decay[0:1, :] * enter_f + start_f[...])
    at_r = (decay[1:2, :] * enter_r + start_r[...], enter_r)
    ones = jnp.ones((8, WIDE), bf16)
    for block in range(2):
        span = slice(block * BLOCK, (block + 1) * BLOCK)
        c_blk = c_rows[span, :]
        base_f, base_r, factor_f, factor_r = (inside0, inside1)[block]
        for way, (state, base, factor) in enumerate(((at_f, base_f, factor_f), (at_r, base_r, factor_r))):
            gated = base[...] + dot(c_blk, state[block].astype(bf16)) * factor[...]
            sums = lax.dot_general(
                ones, (gated * gated).astype(bf16), (((1,), (1,)), ((), ())), preferred_element_type=f32
            )
            for half in range(2):
                at = way * 4 + block * 2 + half
                square[at : at + 1, :] = sums[0:1, half * 128 : (half + 1) * 128]
            gated3[way, 4 * block : 4 * block + 4] = (gated * gain[...]).reshape(4, PIECE, WIDE)
    for slot, mask in enumerate(SLOTS):
        at = me ^ mask
        out_f[slot] = gated3[0, at]
        out_r[slot] = gated3[1, at]
    far[0:PIECE, :] = out_f[7].astype(bf16)
    far[PIECE : 2 * PIECE, :] = out_r[7].astype(bf16)


def gated_outputs(mine, his, other, start_f, start_r, decay, c_rows, inside0, inside1, gain):
    def kernel(a, b, c, d, e, f, g, *refs):
        gated_kernel(a, b, c, d, e, f, g, refs[0:4], refs[4:8], *refs[8:])

    return pl.pallas_call(
        kernel,
        out_shape=[
            jax.ShapeDtypeStruct((8, PIECE, WIDE), f32),
            jax.ShapeDtypeStruct((8, PIECE, WIDE), f32),
            jax.ShapeDtypeStruct((2 * PIECE, WIDE), bf16),
            jax.ShapeDtypeStruct((8, 128), f32),
        ],
        in_specs=vmem(16),
        out_specs=vmem(4),
        scratch_shapes=[pltpu.VMEM((2, 8, PIECE, WIDE), f32)],
        compiler_params=budget(16),
        name="gated_outputs",
    )(mine, his, other, start_f, start_r, decay, c_rows, *inside0, *inside1, gain)


def scale_kernel(gated_f, gated_r, square, *refs):
    outs, scale_out, scale3 = refs[:3], refs[3:6], refs[6]
    me = position()[0]
    scale = lax.rsqrt(square[...] / float(HEADS * HEAD_DIM) + EPSILON)
    columns = jnp.concatenate([scale, jnp.zeros((120, 128), f32)], axis=0).T
    for j in range(4):
        both = jnp.concatenate([columns[:, j : j + 1], columns[:, 4 + j : 5 + j], jnp.zeros((128, 126), f32)], axis=1)
        scale3[2 * j : 2 * j + 2] = both.reshape(2, PIECE, 128)
    slot = 0
    for out in outs:
        for i in range(out.shape[0] // PIECE):
            here = scale3[me ^ SLOTS[slot]]
            if slot >= 4:
                scale_out[slot - 4][...] = here
            out[i * PIECE : (i + 1) * PIECE, :] = (
                gated_f[slot] * here[:, 0:1] + gated_r[slot] * here[:, 1:2]
            ).astype(bf16)
            slot += 1


def scaled_outputs(gated_f, gated_r, square):
    return pl.pallas_call(
        scale_kernel,
        out_shape=[jax.ShapeDtypeStruct((n * PIECE, WIDE), bf16) for n in (1, 3, 3)]
        + [jax.ShapeDtypeStruct((PIECE, 128), f32)] * 3,
        in_specs=vmem(3),
        out_specs=vmem(6),
        scratch_shapes=[pltpu.VMEM((8, PIECE, 128), f32)],
        compiler_params=budget(10),
        name="scaled_outputs",
    )(gated_f, gated_r, square)


def add_part(i, columns, p_mid, arrived, scale):
    rows, columns = slice(i * PIECE, (i + 1) * PIECE), slice(*columns)

    def kernel(p_mid, arrived, scale, out):
        out[...] = p_mid[rows, :].astype(bf16)
        far_f, far_r = arrived[0:PIECE, :].astype(f32), arrived[PIECE : 2 * PIECE, :].astype(f32)
        far = far_f * scale[:, 0:1] + far_r * scale[:, 1:2]
        out[:, columns] = (p_mid[rows, columns] + far).astype(bf16)

    return pl.pallas_call(
        kernel,
        out_shape=jax.ShapeDtypeStruct((PIECE, p_mid.shape[1]), bf16),
        in_specs=vmem(3),
        out_specs=vmem(1)[0],
        compiler_params=budget(4),
    )(p_mid, arrived, scale)


def on_device(
    hidden,
    masked,
    mask_embed,
    in_gain,
    w_gate,
    w_value,
    w_step,
    w_bc,
    dt_bias_forward,
    dt_bias_reverse,
    rate_forward,
    rate_reverse,
    skip_forward,
    skip_reverse,
    out_gain,
    w_out,
):
    own = input_norm(hidden, masked, mask_embed, in_gain)

    def send(dim, array):
        return over(array, dim)

    at_a, at_z, at_b = [send(dim, own) for dim in "AZB"]
    at_za = send("Z", at_a)
    at_bz = send("B", at_z)
    at_ab = send("A", at_b)
    far = [send(dim, array[:, slice(*LAST[dim])]) for dim, array in (("B", at_za), ("A", at_bz))]
    weights = jnp.concatenate([w_value, w_bc, jnp.pad(w_step, ((0, 0), (0, STATE - OWN)))], axis=1)
    proj, gate = [], []
    for i, blocks in enumerate(((own, at_a, at_b, at_z), (at_ab, at_bz, at_za), far), start=1):
        stage = jnp.concatenate(blocks, axis=0 if i < 3 else 1)
        proj.append(dot(stage, weights))
        gate.append(dot(stage, w_gate))

    pay, values, b_rows, c_rows, rows, cols, start_f, start_r, decay = piece_states(
        *proj, dt_bias_forward, dt_bias_reverse, rate_forward, rate_reverse
    )
    mine, his, other = entering_states(pay)
    inside = []
    for block in range(2):
        inside.append(
            inside_block(block, *gate, values, b_rows, c_rows, rows, cols, skip_forward, skip_reverse)
        )
    gated_f, gated_r, far, square = gated_outputs(
        mine, his, other, start_f, start_r, decay, c_rows, *inside, out_gain[None, :]
    )
    p_far = dot(far, w_out).astype(bf16)
    got = {dim: send(dim, p_far[:, slice(*FIRST[dim])]) for dim in "ABZ"}
    for dim in "ABZ":
        square = square + send(dim, square)
    n_own, n_near, n_mid, *scales = scaled_outputs(gated_f, gated_r, square)
    p_mid = dot(n_mid, w_out)

    def with_part(mask, dim):
        return add_part(MID.index(mask), FIRST[dim], p_mid, got[dim], scales[MID.index(mask)])

    got_b = send("A", with_part(2, "Z"))
    got_a = send("Z", with_part(5, "B"))
    got_z = send("B", with_part(7, "A"))
    p_near = dot(n_near, w_out)
    p_near = lax.optimization_barrier([p_near[i * PIECE : (i + 1) * PIECE] for i in range(3)])
    total = lax.optimization_barrier(dot(n_own, w_out))
    near = lambda i, arrived: (p_near[i] + arrived.astype(f32)).astype(bf16)
    total = total + send("Z", near(2, got_z)).astype(f32)
    total = total + send("A", near(0, got_a)).astype(f32)
    total = lax.optimization_barrier(total)
    return (total + send("B", near(1, got_b)).astype(f32)).astype(bf16)


def solution(mesh):
    in_specs = (
        P(("seq", "head"), None),
        P(("seq", "head")),
        P(),
        P(),
        P(None, "head"),
        P(None, "head"),
        P(None, "head"),
        P(),
        P("head"),
        P("head"),
        P("head"),
        P("head"),
        P("head"),
        P("head"),
        P("head"),
        P("head", None),
    )
    out_specs = P(("seq", "head"), None)
    return jax.shard_map(on_device, mesh=mesh, in_specs=in_specs, out_specs=out_specs, check_vma=False)
```
